256 devices in a mesh: gx: 4 (over y_lo, core), gy: 8 (over y_hi, x), gz: 8 (over z).
Axes of the slice: x: 4, y: 4 (y_hi: 2, y_lo: 2; y = y_hi * 2 + y_lo), z: 8, core: 2. Of those that a mesh axis runs over, the one named last changes fastest.
Arguments:
- positions: float32 [4, 8, 8, 3, 1024], P('gx', 'gy', 'gz'), may hold values from 0 to 1
- types: int32 [4, 8, 8, 1024], P('gx', 'gy', 'gz'), may hold values from 0 to 3
- tile_lists: int32 [8, 36], replicated, may hold values from 0 to 215, as said below
- hardness: float32 [4], replicated, may hold values from 2 to 8
- electroneg: float32 [4], replicated, may hold values from 2 to 8
- gamma_table: float32 [4], replicated, may hold values from 0.25 to 1
Outputs:
- charges: float32 [4, 8, 8, 1024], P('gx', 'gy', 'gz')
- solutions: float32 [4, 8, 8, 2, 1024], P('gx', 'gy', 'gz')
The draws below stay inside these ranges and needn't reach their ends.
Inputs may be any that keep to these rules, and one draw needn't show every extreme that they name: `tile_lists`: entry (t, o, u) stands in tile t's list as often as entry (u, 26 - o, t) stands in tile u's list; every offset o of 0 to 26 occurs; the lists are the same for every box.
All inputs are finite; a program needn't handle non-finite values.
Results may differ from the reference program's by a relative error of at most 0.0003.
Values sent between devices are 32-bit elements; how exact they have to be, the bound alone decides.
No kernel may reach another device: no remote copies, remote signals or barrier semaphores. Data moves between devices by JAX's collectives and lax.ppermute only.
A program may use at most 64 MiB of HBM per device.

```python
import math
import jax
import jax.numpy as jnp
from jax import lax

TILES = 8
NBR = 36
NTYPES = 4
ITERS = 4
ATOMS = 1024
BX = 4
BY = 8
BZ = 8


def draw_tile_lists(key, part):
    half = NBR // 2
    first_key = jax.random.fold_in(key, 11)
    second_key = jax.random.fold_in(key, 23)
    orders = jax.vmap(lambda single: jax.random.permutation(single, TILES))(jax.random.split(first_key, half))
    orders = orders.astype(jnp.int32)
    offsets = (jax.random.permutation(second_key, half * TILES).astype(jnp.int32) % 27).reshape(half, TILES)
    forward = offsets * TILES + orders
    inverse = jnp.argsort(orders, axis=1, stable=True).astype(jnp.int32)
    back_offsets = 26 - jnp.take_along_axis(offsets, inverse, axis=1)
    backward = back_offsets * TILES + inverse
    return jnp.concatenate([forward, backward], axis=0).T.astype(jnp.int32)


def with_ends(values, rng, least, high):
    index_at = [jax.random.randint(jax.random.fold_in(rng, axis), (), 0, length) for axis, length in enumerate(values.shape)]
    widest = values.shape.index(max(values.shape))
    next_to = index_at[:widest] + [(index_at[widest] + 1) % values.shape[widest]] + index_at[widest + 1:]
    return values.at[tuple(index_at)].set(least).at[tuple(next_to)].set(high)


def block_scale(key, shape, pieces, low, top_value):
    level = 1.0
    for position, blocks in pieces:
        heights = jax.random.uniform(jax.random.fold_in(jax.random.fold_in(key, 6), position), (blocks,), jnp.float32, low / len(pieces), top_value / len(pieces))
        level = level * jnp.repeat(jnp.exp(heights), shape[position] // blocks).reshape((-1,) + (1,) * (len(shape) - 1 - position))
    return level


def setup_inputs(seed: int = 0) -> dict:
    key_list = jax.random.split(jax.random.key(seed), 7)
    positions = jnp.clip(1.0 * jax.random.uniform(key_list[0], (BX, BY, BZ, 3, ATOMS), jnp.float32) ** block_scale(key_list[0], (BX, BY, BZ, 3, ATOMS), ((0, 4), (1, 8), (2, 8)), -0.2, 0.2), 0.0, 1.0)
    types = with_ends(jax.random.randint(key_list[1], (BX, BY, BZ, ATOMS), 0, NTYPES), jax.random.fold_in(key_list[1], 1), 0, NTYPES - 1).astype(jnp.int32)
    tile_lists = draw_tile_lists(jax.random.fold_in(key_list[6], 71), 0)
    hardness = jnp.clip(jnp.exp(jax.random.uniform(key_list[3], (NTYPES,), jnp.float32, math.log(2.0), math.log(8.0))), 2.0, 8.0)
    electroneg = jnp.clip(jax.random.uniform(key_list[4], (NTYPES,), jnp.float32, 2.0, 8.0), 2.0, 8.0)
    gamma_table = jnp.clip(jnp.exp(jax.random.uniform(key_list[5], (NTYPES,), jnp.float32, math.log(0.25), math.log(1.0))), 0.25, 1.0)
    return {"positions": positions, "types": types, "tile_lists": tile_lists, "hardness": hardness, "electroneg": electroneg, "gamma_table": gamma_table}


CUTOFF = 10.0
COULOMB = 0.3
VOLUME = 10.0

def taper(scaled):
    return scaled ** 4 * (((20.0 * scaled - 70.0) * scaled + 84.0) * scaled - 35.0) + 1.0

def atom_table(types, table):
    kinds = jnp.arange(table.shape[0], dtype=jnp.int32)
    onehot = (types[..., None] == kinds).astype(jnp.float32)
    return jnp.dot(onehot, table, precision=lax.Precision.HIGHEST)

def tile_blocks(nearby, tile_lists, box_edge):
    tile_count = tile_lists.shape[0]
    tile_width = nearby.shape[2]
    local_data = nearby[:, 13 * tile_count:14 * tile_count]
    diagonal_mask = jnp.arange(tile_width)[:, None] == jnp.arange(tile_width)[None, :]

    def one_tile(inputs):
        mine_data, entries, tile_index = inputs
        others = nearby[:, entries]
        offset_box = entries // tile_count
        shifts = jnp.stack([offset_box // 9 - 1, offset_box // 3 % 3 - 1, offset_box % 3 - 1]).astype(jnp.float32)
        separation = (others[:3, :, None, :] + shifts[:, :, None, None] - mine_data[:3, None, :, None]) * box_edge
        spacing = jnp.sqrt(lax.optimization_barrier(jnp.sum(separation * separation, axis=0)))
        present = others[4][:, None, :]
        gamma_other = others[3] + (1.0 - others[4])
        inverse_cube = (mine_data[3][None, :, None] * gamma_other[:, None, :]) ** (-1.5)
        shielding = jnp.cbrt(spacing * spacing * spacing + inverse_cube)
        tapered = jnp.where(spacing < CUTOFF, taper(spacing / CUTOFF), 0.0)
        coupling = COULOMB * tapered / shielding * present
        itself = (entries == 13 * tile_count + tile_index)[:, None, None] & diagonal_mask[None]
        return jnp.where(itself, 0.0, coupling)
    mine_all = jnp.transpose(local_data, (1, 0, 2))
    return lax.map(one_tile, (mine_all, tile_lists, jnp.arange(tile_count, dtype=jnp.int32)))

def couple(blocks, nearby_vectors, tile_lists):
    picked = nearby_vectors[:, tile_lists]
    return jnp.einsum('teij,ktej->kti', blocks, picked, precision=lax.Precision.HIGHEST)

def reference(positions, types, tile_lists, hardness, electroneg, gamma_table):
    grid = positions.shape[:3]
    atoms = positions.shape[4]
    tile_count = tile_lists.shape[0]
    tile_width = atoms // tile_count
    box_edge = (atoms * VOLUME) ** (1.0 / 3.0)
    hardness_atom = atom_table(types, hardness)
    electro_atom = atom_table(types, electroneg)
    gamma_atom = atom_table(types, gamma_table)
    present = jnp.ones_like(gamma_atom)
    atom_data = jnp.concatenate([positions, gamma_atom[:, :, :, None], present[:, :, :, None]], axis=3)
    box_total = grid[0] * grid[1] * grid[2]
    box_ids = jnp.arange(box_total, dtype=jnp.int32)

    def padding(field):
        return jnp.pad(field, ((1, 1), (1, 1), (1, 1), (0, 0), (0, 0)))

    def gather_box(padded, box):
        first = (box // (grid[1] * grid[2])).astype(jnp.int32)
        second = (box // grid[2] % grid[1]).astype(jnp.int32)
        third = (box % grid[2]).astype(jnp.int32)
        anchor = jnp.zeros((), jnp.int32)
        piece = lax.dynamic_slice(padded, (first, second, third, anchor, anchor), (3, 3, 3) + padded.shape[3:])
        channels = padded.shape[3]
        arranged = jnp.transpose(piece.reshape(27, channels, tile_count, tile_width), (1, 0, 2, 3))
        return arranged.reshape(channels, 27 * tile_count, tile_width)
    padded_data = padding(atom_data)

    def box_blocks(box):
        return tile_blocks(gather_box(padded_data, box), tile_lists, box_edge)
    blocks = lax.map(box_blocks, box_ids)

    def apply(vectors):
        padded = padding(vectors)
        systems = vectors.shape[3]

        def one_box(inputs):
            box_matrix, box = inputs
            return couple(box_matrix, gather_box(padded, box), tile_lists).reshape(systems, atoms)
        coupled = lax.map(one_box, (blocks, box_ids)).reshape(vectors.shape)
        return hardness_atom[:, :, :, None, :] * vectors + coupled

    def total(field):
        return lax.optimization_barrier(jnp.sum(field, axis=(0, 1, 2, 4)))[:, None]
    right = jnp.stack([-electro_atom, -jnp.ones_like(electro_atom)], axis=3)
    solution = jnp.zeros_like(right)
    residual = right
    direction = right
    norm_now = total(residual * residual)
    for iteration in range(ITERS):
        image = apply(direction)
        alpha = norm_now / total(direction * image)
        solution = solution + alpha * direction
        residual = residual - alpha * image
        norm_next = total(residual * residual)
        direction = residual + norm_next / norm_now * direction
        norm_now = norm_next
    sums = lax.optimization_barrier(jnp.sum(solution, axis=(0, 1, 2, 4)))
    charges = solution[:, :, :, 0] - sums[0] / sums[1] * solution[:, :, :, 1]
    return (charges, solution)
```

```python
import functools

import jax
import jax.numpy as jnp
import numpy as np
from jax import lax
from jax.experimental import pallas as pl
from jax.experimental.pallas import tpu as pltpu
from jax.sharding import PartitionSpec as P

ITERS = 4
CUTOFF = 10.0
COULOMB = 0.3
VOLUME = 10.0
TILES = 8
W = 128
F32 = jnp.float32
BF16 = jnp.bfloat16
MIB = 1 << 20
FAR = 1e4
DROP = 1e-9

OFFSETS = np.array([(i % 3 - 1, i // 3 % 3 - 1, i // 9 - 1) for i in range(27)])
HOME = 13
ROWS = 27 * TILES
ENTRIES = 18

VMEM = pl.BlockSpec(memory_space=pltpu.VMEM)
SMEM = pl.BlockSpec(memory_space=pltpu.SMEM)


def surrounded(cells):
    cells = cells[None]
    for axis in ("gx", "gy", "gz"):
        count = lax.axis_size(axis)
        before = lax.ppermute(cells, axis, [(i, (i + 1) % count) for i in range(count)])
        after = lax.ppermute(cells, axis, [((i + 1) % count, i) for i in range(count)])
        cells = jnp.concatenate([before, cells, after], axis=0)
    return cells


def summed(rows):
    for axis in ("gx", "gy", "gz"):
        count = lax.axis_size(axis)
        step = 1
        while step < count:
            rows = rows + lax.ppermute(rows, axis, [(i, i ^ step) for i in range(count)])
            step *= 2
    return rows


def pieces(value):
    high = value.astype(BF16).astype(F32)
    rest = value - high
    middle = rest.astype(BF16).astype(F32)
    return high, middle, rest - middle


def by_kind(kind, table):
    return jnp.where(
        kind < 0.5,
        table[0],
        jnp.where(kind < 1.5, table[1], jnp.where(kind < 2.5, table[2], table[3])),
    )


def build_kernel(edge, lists, far, powers, electro, near, blocks, start, others, others_p, own, floor):
    zero = jnp.zeros((TILES, W), F32)
    one = jnp.ones((TILES, W), F32)

    def atoms(box):
        place = [
            (near[box, 8 * k : 8 * k + 8, :] + (float(OFFSETS[box][k]) - 0.5)) * edge
            for k in range(3)
        ]
        kind = near[box, 24:32, :]
        square = place[0] * place[0] + place[1] * place[1] + place[2] * place[2]
        return place, kind, by_kind(kind, powers), square

    for box in range(27):
        place, kind, power, square = atoms(box)
        rows = []
        for value in place:
            high, middle, low = pieces(value)
            rows += [high, middle, high, middle, low, high]
        rows += [one, one, one] + list(pieces(square + far[box])) + [zero] * 8
        for k, row in enumerate(rows):
            others[k * ROWS + box * 8 : k * ROWS + box * 8 + 8, :] = row
        high, middle, _ = pieces(power)
        for k, row in enumerate([high, middle, high] + [zero] * 5):
            others_p[k * ROWS + box * 8 : k * ROWS + box * 8 + 8, :] = row
        start[16 * box : 16 * box + 8, :] = -by_kind(kind, electro)
        start[16 * box + 8 : 16 * box + 16, :] = -one
    place, kind, power, square = atoms(HOME)
    rows = []
    for value in place:
        high, middle, low = pieces(-2.0 * value)
        rows += [high, high, middle, middle, high, low]
    rows += list(pieces(square)) + [one, one, one]
    high, middle, _ = pieces(power)
    rows += [high, high, middle] + [zero] * (W - 27)
    for k, row in enumerate(rows):
        own[k * 8 : k * 8 + 8, :] = row
    diagonal = lax.broadcasted_iota(jnp.int32, (W, W), 0) == lax.broadcasted_iota(
        jnp.int32, (W, W), 1
    )
    floor[0] = jnp.full((W, W), 1e-12, F32)
    floor[1] = jnp.where(diagonal, 2.0, 1e-12)
    blank = jnp.zeros((24, W), BF16)

    def tile(t, carry):
        left = jnp.transpose(own[pl.ds(t, W, stride=8), :])[:, :32].astype(BF16)

        def entry(e, carry):
            which = lists[t, e]
            right = others[pl.ds(which, 32, stride=ROWS), :].astype(BF16)
            right_p = others_p[pl.ds(which, 8, stride=ROWS), :].astype(BF16)
            right = jnp.concatenate([right, jnp.concatenate([blank, right_p], axis=0)], axis=1)
            both = lax.dot_general(
                left, right, (((1,), (0,)), ((), ())), preferred_element_type=F32
            )
            least = floor[jnp.where(which == HOME * TILES + t, 1, 0)]
            square = jnp.minimum(jnp.maximum(both[:, :W], least), 1.0)
            length = square * lax.rsqrt(square)
            cube = length * square + both[:, W:]
            shield = jnp.exp2(jnp.log2(cube) * (-1.0 / 3.0))
            gap = 1.0 - length
            gap = gap * gap
            shape = (length + 0.5) * (square + 0.2) - 0.05
            blocks[t, e] = (gap * gap) * (shape * shield)
            return carry

        return lax.fori_loop(0, lists.shape[1], entry, carry, unroll=4)

    lax.fori_loop(0, TILES, tile, 0)


def build(lists, far, powers, electro, near, edge):
    entries = lists.shape[1]
    return pl.pallas_call(
        functools.partial(build_kernel, edge),
        out_shape=(
            pltpu.VMEM((TILES, entries, W, W), F32),
            jax.ShapeDtypeStruct((27 * 16, W), F32),
        ),
        in_specs=[SMEM, SMEM, SMEM, SMEM, VMEM],
        out_specs=(VMEM, VMEM),
        scratch_shapes=[
            pltpu.VMEM((32 * ROWS, W), F32),
            pltpu.VMEM((8 * ROWS, W), F32),
            pltpu.VMEM((8 * W, W), F32),
            pltpu.VMEM((2, W, W), F32),
        ],
        compiler_params=pltpu.CompilerParams(vmem_limit_bytes=8 * MIB),
        name="build",
    )(lists, far, powers, electro, near)


def product_kernel(last, lists, scalars, around, kinds, blocks, *rest):
    earlier, (out, total) = rest[:-2], rest[-2:]

    def tile(t, carry):
        def entry(e, sums):
            which = lists[t, e]
            row = which // TILES * 16 + which % TILES
            block = blocks[t, e]
            return (
                sums[0] + block * around[pl.ds(row, 1), :],
                sums[1] + block * around[pl.ds(row + 8, 1), :],
            )

        zero = jnp.zeros((W, W), F32)
        sums = lax.fori_loop(0, lists.shape[1], entry, (zero, zero), unroll=2)
        for k in range(2):
            total[pl.ds(t + 8 * k, 1), :] = jnp.sum(jnp.transpose(sums[k]), axis=0, keepdims=True)
        return carry

    lax.fori_loop(0, TILES, tile, 0)
    kind = kinds[...]
    eta = by_kind(kind, [scalars[2 + k] for k in range(4)])
    home = around[16 * HOME : 16 * HOME + 16, :]
    following = total[...] * scalars[0] + jnp.concatenate([eta, eta], axis=0) * home
    if not last:
        out[...] = following
        return
    basis = [ref[...] for ref in earlier] + [home, following]
    for k in range(2):
        parts = [v[8 * k : 8 * k + 8] for v in basis]
        rows = [parts[i] * parts[j] for i in range(ITERS) for j in range(i, ITERS + 1)] + parts[:ITERS]
        for index, row in enumerate(rows):
            out[2 * index + k : 2 * index + k + 1, :] = jnp.sum(row, axis=0, keepdims=True)
    out[36:40, :] = jnp.zeros((4, W), F32)


def product(lists, scalars, around, kinds, blocks, earlier=()):
    last = bool(earlier)
    return pl.pallas_call(
        functools.partial(product_kernel, last),
        out_shape=jax.ShapeDtypeStruct((40 if last else 16, W), F32),
        in_specs=[SMEM, SMEM, VMEM, VMEM, VMEM] + [VMEM] * len(earlier),
        out_specs=VMEM,
        scratch_shapes=[pltpu.VMEM((16, W), F32)],
        compiler_params=pltpu.CompilerParams(vmem_limit_bytes=8 * MIB),
        name="product",
    )(lists, scalars, around, kinds, blocks, *earlier)


def two_sum(a, b):
    s = a + b
    t = s - a
    return s, (a - (s - t)) + (b - t)


def halves(a):
    t = a * 4097.0
    high = t - (t - a)
    return high, a - high


def add(a, b):
    s, e = two_sum(a[0], b[0])
    return two_sum(s, e + (a[1] + b[1]))


def mul(a, b):
    p = a[0] * b[0]
    ah, al = halves(a[0])
    bh, bl = halves(b[0])
    e = ((ah * bh - p) + ah * bl + al * bh) + al * bl
    return two_sum(p, e + (a[0] * b[1] + a[1] * b[0]))


def neg(a):
    return -a[0], -a[1]


def inverse(a):
    y = 1.0 / a[0]
    guess = (y, jnp.zeros_like(y))
    slip = add((jnp.ones_like(y), jnp.zeros_like(y)), neg(mul(a, guess)))
    return add(guess, mul(guess, slip))


def finish_kernel(scalars, gram, v0, v1, v2, v3, charges, solutions):
    pair = (gram[...], jnp.zeros((40, W), F32))
    shift = W // 2
    while shift:
        pair = add(pair, (pltpu.roll(pair[0], shift, 1), pltpu.roll(pair[1], shift, 1)))
        shift //= 2

    def value(index):
        return pair[0][2 * index : 2 * index + 2], pair[1][2 * index : 2 * index + 2]

    index_of = {}
    for i in range(ITERS):
        for j in range(i, ITERS + 1):
            index_of[i, j] = len(index_of)
    dots = {key: value(index) for key, index in index_of.items()}
    sums = [value(len(index_of) + i) for i in range(ITERS)]

    def dot(i, j):
        return dots[min(i, j), max(i, j)]

    none = jnp.zeros((2, W), F32)
    spread = (jnp.full((2, W), scalars[6], F32), none)
    centre = (jnp.full((2, W), scalars[7], F32), none)
    matrix = {
        (i, j): add(mul(spread, dot(i, j + 1)), mul(centre, dot(i, j)))
        for i in range(ITERS)
        for j in range(i + 1)
    }
    size = [abs(matrix[i, i][0]) for i in range(ITERS)]
    right = [dot(i, 0) for i in range(ITERS)]
    inverses, factors = [], {}
    for k in range(ITERS):
        pivot = matrix[k, k]
        usable = abs(pivot[0]) > DROP * size[k]
        turned = inverse((jnp.where(usable, pivot[0], 1.0), jnp.where(usable, pivot[1], 0.0)))
        turned = (jnp.where(usable, turned[0], 0.0), jnp.where(usable, turned[1], 0.0))
        inverses.append(turned)
        for i in range(k + 1, ITERS):
            factors[i, k] = mul(matrix[i, k], turned)
        for i in range(k + 1, ITERS):
            for j in range(k + 1, i + 1):
                matrix[i, j] = add(matrix[i, j], neg(mul(factors[i, k], matrix[j, k])))
            right[i] = add(right[i], neg(mul(factors[i, k], right[k])))
    weights = [None] * ITERS
    for k in reversed(range(ITERS)):
        weight = mul(right[k], inverses[k])
        for i in range(k + 1, ITERS):
            weight = add(weight, neg(mul(factors[i, k], weights[i])))
        weights[k] = weight
    whole = mul(weights[0], sums[0])
    for k in range(1, ITERS):
        whole = add(whole, mul(weights[k], sums[k]))
    basis = [ref[...] for ref in (v0, v1, v2, v3)]
    parts = []
    for k in range(2):
        part = weights[0][0][k : k + 1] * basis[0][8 * k : 8 * k + 8]
        for i in range(1, ITERS):
            part = part + weights[i][0][k : k + 1] * basis[i][8 * k : 8 * k + 8]
        parts.append(part)
        solutions[8 * k : 8 * k + 8, :] = part
    level = whole[0][0:1] / whole[0][1:2]
    charges[...] = parts[0] - level * parts[1]


def finish(scalars, gram, basis):
    return pl.pallas_call(
        finish_kernel,
        out_shape=(jax.ShapeDtypeStruct((TILES, W), F32), jax.ShapeDtypeStruct((16, W), F32)),
        in_specs=[SMEM] + [VMEM] * 5,
        out_specs=(VMEM, VMEM),
        compiler_params=pltpu.CompilerParams(vmem_limit_bytes=8 * MIB),
        name="finish",
    )(scalars, gram, *basis)


def on_device(positions, types, tile_lists, hardness, electroneg, gamma_table):
    atoms = positions.shape[4]
    edge = (atoms * VOLUME) ** (1.0 / 3.0) / CUTOFF
    box = tile_lists // TILES
    place = (box % 3) * 9 + box // 3 % 3 * 3 + box // 9
    lists = place * TILES + tile_lists % TILES
    inside = jnp.ones((27,), bool)
    for k, axis in enumerate(("gx", "gy", "gz")):
        there = lax.axis_index(axis) + OFFSETS[:, k].astype(np.int32)
        inside = inside & (there >= 0) & (there < lax.axis_size(axis))
    far = jnp.where(inside, 0.0, FAR).astype(F32)
    powers = gamma_table**-1.5 * CUTOFF**-1.5
    least, most = jnp.min(hardness), jnp.max(hardness)
    centre = 0.5 * (least + most) + 1.0
    spread = 0.5 * (most - least) + 1.5
    scale = 20.0 * COULOMB / CUTOFF
    scalars = jnp.concatenate(
        [
            jnp.stack([scale / spread, 1.0 / spread]),
            (hardness - centre) / spread,
            jnp.stack([spread, centre]),
        ]
    )
    kinds = types.reshape(TILES, W).astype(F32)
    cells = jnp.concatenate([positions.reshape(3 * TILES, W), kinds], axis=0)
    near = surrounded(cells)
    blocks, start = build(lists, far, powers, electroneg, near, edge)
    basis = [start[16 * HOME : 16 * HOME + 16]]
    around = start
    for _ in range(ITERS - 1):
        basis.append(product(lists, scalars, around, kinds, blocks))
        around = surrounded(basis[-1]).reshape(27 * 16, W)
    gram = summed(product(lists, scalars, around, kinds, blocks, tuple(basis[:-1])))
    charges, solutions = finish(scalars, gram, basis)
    return charges.reshape(1, 1, 1, atoms), solutions.reshape(1, 1, 1, 2, atoms)


def solution(mesh):
    across = ("gx", "gy", "gz")
    return jax.shard_map(
        on_device,
        mesh=mesh,
        in_specs=(P(*across, None, None), P(*across, None), P(), P(), P(), P()),
        out_specs=(P(*across, None), P(*across, None, None)),
        check_vma=False,
    )
```

```python
import functools

import jax
import jax.numpy as jnp
import numpy as np
from jax import lax
from jax.experimental import pallas as pl
from jax.experimental.pallas import tpu as pltpu
from jax.sharding import Mesh
from jax.sharding import PartitionSpec as P

ITERS = 4
AXES = (("y_low", "core"), ("y_high", "x"), "gz")
CUTOFF = 10.0
COULOMB = 0.3
VOLUME = 10.0
TILES = 8
W = 128
F32 = jnp.float32
BF16 = jnp.bfloat16
MIB = 1 << 20
FAR = 1e4
DROP = 1e-9

OFFSETS = np.array([(i % 3 - 1, i // 3 % 3 - 1, i // 9 - 1) for i in range(27)])
HOME = 13
ROWS = 27 * TILES
ENTRIES = 18
LINES = 5

VMEM = pl.BlockSpec(memory_space=pltpu.VMEM)
SMEM = pl.BlockSpec(memory_space=pltpu.SMEM)


def surrounded(cells):
    cells = cells[None]
    for axis in AXES:
        count = lax.axis_size(axis)
        before = lax.ppermute(cells, axis, [(i, (i + 1) % count) for i in range(count)])
        after = lax.ppermute(cells, axis, [((i + 1) % count, i) for i in range(count)])
        cells = jnp.concatenate([before, cells, after], axis=0)
    return cells


def met(rows, axis, count, steps):
    parts = [rows] + [
        lax.ppermute(rows, axis, [(i, i ^ step) for i in range(count)]) for step in steps
    ]
    while len(parts) > 1:
        parts = [parts[i] + parts[i + 1] for i in range(0, len(parts), 2)]
    return parts[0]


def summed(rows):
    rows = met(rows, "core", 2, (1,))
    rows = met(rows, ("y_low", "y_high"), 4, (1, 2, 3))
    rows = met(rows, "x", 4, (1, 2, 3))
    for steps in ((1, 2, 3), (4,)):
        rows = met(rows, "gz", 8, steps)
    return rows


def pieces(value):
    high = value.astype(BF16).astype(F32)
    rest = value - high
    middle = rest.astype(BF16).astype(F32)
    return high, middle, rest - middle


def by_kind(kind, table):
    return jnp.where(
        kind < 0.5,
        table[0],
        jnp.where(kind < 1.5, table[1], jnp.where(kind < 2.5, table[2], table[3])),
    )


def build_kernel(edge, lists, far, powers, electro, near, blocks, start, others, others_p, own, floor):
    zero = jnp.zeros((TILES, W), F32)
    one = jnp.ones((TILES, W), F32)

    def atoms(box):
        place = [
            (near[box, 8 * k : 8 * k + 8, :] + (float(OFFSETS[box][k]) - 0.5)) * edge
            for k in range(3)
        ]
        kind = near[box, 24:32, :]
        square = place[0] * place[0] + place[1] * place[1] + place[2] * place[2]
        return place, kind, by_kind(kind, powers), square

    for box in range(27):
        place, kind, power, square = atoms(box)
        rows = []
        for value in place:
            high, middle, low = pieces(value)
            rows += [high, middle, high, middle, low, high]
        rows += [one, one, one] + list(pieces(square + far[box])) + [zero] * 8
        for k, row in enumerate(rows):
            others[k * ROWS + box * 8 : k * ROWS + box * 8 + 8, :] = row
        high, middle, _ = pieces(power)
        for k, row in enumerate([high, middle, high] + [zero] * 5):
            others_p[k * ROWS + box * 8 : k * ROWS + box * 8 + 8, :] = row
        start[16 * box : 16 * box + 8, :] = -by_kind(kind, electro)
        start[16 * box + 8 : 16 * box + 16, :] = -one
    place, kind, power, square = atoms(HOME)
    rows = []
    for value in place:
        high, middle, low = pieces(-2.0 * value)
        rows += [high, high, middle, middle, high, low]
    rows += list(pieces(square)) + [one, one, one]
    high, middle, _ = pieces(power)
    rows += [high, high, middle] + [zero] * (W - 27)
    for k, row in enumerate(rows):
        own[k * 8 : k * 8 + 8, :] = row
    diagonal = lax.broadcasted_iota(jnp.int32, (W, W), 0) == lax.broadcasted_iota(
        jnp.int32, (W, W), 1
    )
    floor[0] = jnp.full((W, W), 1e-12, F32)
    floor[1] = jnp.where(diagonal, 2.0, 1e-12)
    blank = jnp.zeros((24, W), BF16)

    def tile(t, carry):
        left = jnp.transpose(own[pl.ds(t, W, stride=8), :])[:, :32].astype(BF16)

        def entry(e, carry):
            which = lists[t, e]
            right = others[pl.ds(which, 32, stride=ROWS), :].astype(BF16)
            right_p = others_p[pl.ds(which, 8, stride=ROWS), :].astype(BF16)
            right = jnp.concatenate([right, jnp.concatenate([blank, right_p], axis=0)], axis=1)
            both = lax.dot_general(
                left, right, (((1,), (0,)), ((), ())), preferred_element_type=F32
            )
            least = floor[jnp.where(which == HOME * TILES + t, 1, 0)]
            square = jnp.minimum(jnp.maximum(both[:, :W], least), 1.0)
            length = square * lax.rsqrt(square)
            cube = length * square + both[:, W:]
            shield = jnp.exp2(jnp.log2(cube) * (-1.0 / 3.0))
            gap = 1.0 - length
            gap = gap * gap
            shape = (length + 0.5) * (square + 0.2) - 0.05
            blocks[t, e] = (gap * gap) * (shape * shield)
            return carry

        return lax.fori_loop(0, lists.shape[1], entry, carry, unroll=36)

    lax.fori_loop(0, TILES, tile, 0)


def build(lists, far, powers, electro, near, edge):
    entries = lists.shape[1]
    return pl.pallas_call(
        functools.partial(build_kernel, edge),
        out_shape=(
            pltpu.VMEM((TILES, entries, W, W), F32),
            jax.ShapeDtypeStruct((27 * 16, W), F32),
        ),
        in_specs=[SMEM, SMEM, SMEM, SMEM, VMEM],
        out_specs=(VMEM, VMEM),
        scratch_shapes=[
            pltpu.VMEM((32 * ROWS, W), F32),
            pltpu.VMEM((8 * ROWS, W), F32),
            pltpu.VMEM((8 * W, W), F32),
            pltpu.VMEM((2, W, W), F32),
        ],
        compiler_params=pltpu.CompilerParams(vmem_limit_bytes=8 * MIB),
        name="build",
    )(lists, far, powers, electro, near)


def own_lanes():
    shape = (LINES, 8, W)
    return lax.broadcasted_iota(jnp.int32, shape, 2) // 16 == lax.broadcasted_iota(
        jnp.int32, shape, 1
    )


def product_kernel(last, lists, scalars, around, kinds, blocks, *rest):
    earlier, (out, total, table) = rest[:-3], rest[-3:]

    def tile(t, carry):
        def entry(e, sums):
            at = lists[t, e]
            block = blocks[t, e].reshape(W // 8, 8, W)
            return tuple(
                sums[k] + block * around[pl.ds(at + 8 * k, 8, stride=0), :][None]
                for k in range(2)
            )

        zero = jnp.zeros((W // 8, 8, W), F32)
        sums = lax.fori_loop(0, lists.shape[1], entry, (zero, zero), unroll=12)
        for k in range(2):
            turned = jnp.transpose(sums[k].reshape(W, W))
            total[pl.ds(t + 8 * k, 1), :] = jnp.sum(turned, axis=0, keepdims=True)
        return carry

    lax.fori_loop(0, TILES, tile, 0)
    kind = kinds[...]
    eta = by_kind(kind, [scalars[2 + k] for k in range(4)])
    home = around[16 * HOME : 16 * HOME + 16, :]
    following = total[...] * scalars[0] + jnp.concatenate([eta, eta], axis=0) * home
    if not last:
        out[...] = following
        return
    basis = [ref[...] for ref in earlier] + [home, following]
    for k in range(2):
        parts = [v[8 * k : 8 * k + 8] for v in basis]
        rows = [parts[i] * parts[j] for i in range(ITERS) for j in range(i, ITERS + 1)] + parts[:ITERS]
        for index, row in enumerate(rows):
            table[2 * index + k : 2 * index + k + 1, :] = jnp.sum(row, axis=0, keepdims=True)
    table[2 * ENTRIES :, :] = jnp.zeros((LINES * 8 - 2 * ENTRIES, W), F32)
    folded = table[...]
    for shift in (64, 32, 16):
        folded = folded + pltpu.roll(folded, shift, 1)
    kept = jnp.where(own_lanes(), folded.reshape(LINES, 8, W), 0.0)
    out[:LINES, :] = jnp.sum(kept, axis=1)
    out[LINES:, :] = jnp.zeros((8 - LINES, W), F32)


def product(lists, scalars, around, kinds, blocks, earlier=()):
    last = bool(earlier)
    return pl.pallas_call(
        functools.partial(product_kernel, last),
        out_shape=jax.ShapeDtypeStruct((8 if last else 16, W), F32),
        in_specs=[SMEM, SMEM, VMEM, VMEM, VMEM] + [VMEM] * len(earlier),
        out_specs=VMEM,
        scratch_shapes=[pltpu.VMEM((16, W), F32), pltpu.VMEM((LINES * 8, W), F32)],
        compiler_params=pltpu.CompilerParams(vmem_limit_bytes=8 * MIB),
        name="product",
    )(lists, scalars, around, kinds, blocks, *earlier)


def two_sum(a, b):
    s = a + b
    t = s - a
    return s, (a - (s - t)) + (b - t)


def halves(a):
    t = a * 4097.0
    high = t - (t - a)
    return high, a - high


def add(a, b):
    s, e = two_sum(a[0], b[0])
    return two_sum(s, e + (a[1] + b[1]))


def mul(a, b):
    p = a[0] * b[0]
    ah, al = halves(a[0])
    bh, bl = halves(b[0])
    e = ((ah * bh - p) + ah * bl + al * bh) + al * bl
    return two_sum(p, e + (a[0] * b[1] + a[1] * b[0]))


def neg(a):
    return -a[0], -a[1]


def inverse(a):
    y = 1.0 / a[0]
    guess = (y, jnp.zeros_like(y))
    slip = add((jnp.ones_like(y), jnp.zeros_like(y)), neg(mul(a, guess)))
    return add(guess, mul(guess, slip))


def finish_kernel(scalars, gram, v0, v1, v2, v3, charges, solutions):
    spread_out = jnp.broadcast_to(gram[:LINES, :][:, None, :], (LINES, 8, W))
    pair = (jnp.where(own_lanes(), spread_out, 0.0).reshape(LINES * 8, W),)
    pair += (jnp.zeros((LINES * 8, W), F32),)
    shift = W // 2
    while shift:
        pair = add(pair, (pltpu.roll(pair[0], shift, 1), pltpu.roll(pair[1], shift, 1)))
        shift //= 2

    def value(index):
        return pair[0][2 * index : 2 * index + 2], pair[1][2 * index : 2 * index + 2]

    index_of = {}
    for i in range(ITERS):
        for j in range(i, ITERS + 1):
            index_of[i, j] = len(index_of)
    dots = {key: value(index) for key, index in index_of.items()}
    sums = [value(len(index_of) + i) for i in range(ITERS)]

    def dot(i, j):
        return dots[min(i, j), max(i, j)]

    none = jnp.zeros((2, W), F32)
    spread = (jnp.full((2, W), scalars[6], F32), none)
    centre = (jnp.full((2, W), scalars[7], F32), none)
    matrix = {
        (i, j): add(mul(spread, dot(i, j + 1)), mul(centre, dot(i, j)))
        for i in range(ITERS)
        for j in range(i + 1)
    }
    size = [abs(matrix[i, i][0]) for i in range(ITERS)]
    right = [dot(i, 0) for i in range(ITERS)]
    inverses, factors = [], {}
    for k in range(ITERS):
        pivot = matrix[k, k]
        usable = abs(pivot[0]) > DROP * size[k]
        turned = inverse((jnp.where(usable, pivot[0], 1.0), jnp.where(usable, pivot[1], 0.0)))
        turned = (jnp.where(usable, turned[0], 0.0), jnp.where(usable, turned[1], 0.0))
        inverses.append(turned)
        for i in range(k + 1, ITERS):
            factors[i, k] = mul(matrix[i, k], turned)
        for i in range(k + 1, ITERS):
            for j in range(k + 1, i + 1):
                matrix[i, j] = add(matrix[i, j], neg(mul(factors[i, k], matrix[j, k])))
            right[i] = add(right[i], neg(mul(factors[i, k], right[k])))
    weights = [None] * ITERS
    for k in reversed(range(ITERS)):
        weight = mul(right[k], inverses[k])
        for i in range(k + 1, ITERS):
            weight = add(weight, neg(mul(factors[i, k], weights[i])))
        weights[k] = weight
    whole = mul(weights[0], sums[0])
    for k in range(1, ITERS):
        whole = add(whole, mul(weights[k], sums[k]))
    basis = [ref[...] for ref in (v0, v1, v2, v3)]
    parts = []
    for k in range(2):
        part = weights[0][0][k : k + 1] * basis[0][8 * k : 8 * k + 8]
        for i in range(1, ITERS):
            part = part + weights[i][0][k : k + 1] * basis[i][8 * k : 8 * k + 8]
        parts.append(part)
        for u in range(TILES):
            solutions[u, k : k + 1, :] = part[u : u + 1]
    level = whole[0][0:1] / whole[0][1:2]
    charges[...] = parts[0] - level * parts[1]


def finish(scalars, gram, basis):
    return pl.pallas_call(
        finish_kernel,
        out_shape=(jax.ShapeDtypeStruct((TILES, W), F32), jax.ShapeDtypeStruct((TILES, 2, W), F32)),
        in_specs=[SMEM] + [VMEM] * 5,
        out_specs=(VMEM, VMEM),
        compiler_params=pltpu.CompilerParams(vmem_limit_bytes=8 * MIB),
        name="finish",
    )(scalars, gram, *basis)


def on_device(positions, types, tile_lists, hardness, electroneg, gamma_table):
    atoms = positions.shape[4]
    edge = (atoms * VOLUME) ** (1.0 / 3.0) / CUTOFF
    box = tile_lists // TILES
    place = (box % 3) * 9 + box // 3 % 3 * 3 + box // 9
    lists = place * TILES + tile_lists % TILES
    rows = place * 2 * TILES + tile_lists % TILES
    inside = jnp.ones((27,), bool)
    for k, axis in enumerate(AXES):
        there = lax.axis_index(axis) + OFFSETS[:, k].astype(np.int32)
        inside = inside & (there >= 0) & (there < lax.axis_size(axis))
    far = jnp.where(inside, 0.0, FAR).astype(F32)
    powers = gamma_table**-1.5 * CUTOFF**-1.5
    least, most = jnp.min(hardness), jnp.max(hardness)
    centre = 0.5 * (least + most) + 1.0
    spread = 0.5 * (most - least) + 1.5
    scale = 20.0 * COULOMB / CUTOFF
    scalars = jnp.concatenate(
        [
            jnp.stack([scale / spread, 1.0 / spread]),
            (hardness - centre) / spread,
            jnp.stack([spread, centre]),
        ]
    )
    kinds = types.reshape(TILES, W).astype(F32)
    cells = jnp.concatenate([positions.reshape(3 * TILES, W), kinds], axis=0)
    near = surrounded(cells)
    blocks, start = build(lists, far, powers, electroneg, near, edge)
    basis = [start[16 * HOME : 16 * HOME + 16]]
    around = start
    for _ in range(ITERS - 1):
        basis.append(product(rows, scalars, around, kinds, blocks))
        around = surrounded(basis[-1]).reshape(27 * 16, W)
    gram = summed(product(rows, scalars, around, kinds, blocks, tuple(basis[:-1])))
    charges, solutions = finish(scalars, gram, basis)
    solutions = jnp.transpose(solutions, (1, 0, 2)).reshape(1, 1, 1, 2, atoms)
    return charges.reshape(1, 1, 1, atoms), solutions


def solution(mesh):
    names = ("y_low", "core", "y_high", "x", "gz")
    split = Mesh(mesh.devices.reshape(2, 2, 2, 4, mesh.shape["gz"]), names)
    return jax.shard_map(
        on_device,
        mesh=split,
        in_specs=(P(*AXES, None, None), P(*AXES, None), P(), P(), P(), P()),
        out_specs=(P(*AXES, None), P(*AXES, None, None)),
        check_vma=False,
    )
```

```python
import functools

import jax
import jax.numpy as jnp
import numpy as np
from jax import lax
from jax.experimental import pallas as pl
from jax.experimental.pallas import tpu as pltpu
from jax.sharding import Mesh
from jax.sharding import PartitionSpec as P

ITERS = 4
AXES = (("y_low", "core"), ("y_high", "x"), "gz")
CUTOFF = 10.0
COULOMB = 0.3
VOLUME = 10.0
TILES = 8
W = 128
F32 = jnp.float32
BF16 = jnp.bfloat16
MIB = 1 << 20
FAR = 1e4
DROP = 1e-9

OFFSETS = np.array([(i % 3 - 1, i // 3 % 3 - 1, i // 9 - 1) for i in range(27)])
HOME = 13
ROWS = 27 * TILES
ENTRIES = 18
LINES = 5

VMEM = pl.BlockSpec(memory_space=pltpu.VMEM)
SMEM = pl.BlockSpec(memory_space=pltpu.SMEM)


def surrounded(cells):
    cells = cells[None]
    for axis in AXES:
        count = lax.axis_size(axis)
        before = lax.ppermute(cells, axis, [(i, (i + 1) % count) for i in range(count)])
        after = lax.ppermute(cells, axis, [((i + 1) % count, i) for i in range(count)])
        cells = jnp.concatenate([before, cells, after], axis=0)
    return cells


def met(rows, axis, count, steps):
    parts = [rows] + [
        lax.ppermute(rows, axis, [(i, i ^ step) for i in range(count)]) for step in steps
    ]
    while len(parts) > 1:
        parts = [parts[i] + parts[i + 1] for i in range(0, len(parts), 2)]
    return parts[0]


def summed(rows):
    rows = met(rows, "core", 2, (1,))
    rows = met(rows, ("y_low", "y_high"), 4, (1, 2, 3))
    rows = met(rows, "x", 4, (1, 2, 3))
    for steps in ((1, 2, 3), (4,)):
        rows = met(rows, "gz", 8, steps)
    return rows


def pieces(value):
    high = value.astype(BF16).astype(F32)
    rest = value - high
    middle = rest.astype(BF16).astype(F32)
    return high, middle, rest - middle


def by_kind(kind, table):
    return jnp.where(
        kind < 0.5,
        table[0],
        jnp.where(kind < 1.5, table[1], jnp.where(kind < 2.5, table[2], table[3])),
    )


def build_kernel(edge, lists, far, table, near, blocks, start, others, others_p, own, floor):
    zero = jnp.zeros((TILES, W), F32)
    one = jnp.ones((TILES, W), F32)

    def atoms(box):
        place = [
            (near[box, 8 * k : 8 * k + 8, :] + (float(OFFSETS[box][k]) - 0.5)) * edge
            for k in range(3)
        ]
        kind = near[box, 24:32, :]
        square = place[0] * place[0] + place[1] * place[1] + place[2] * place[2]
        root = lax.rsqrt(by_kind(kind, [table[8 + k] for k in range(4)]))
        power = root * root * root * CUTOFF**-1.5
        return place, kind, power, square

    for box in range(27):
        place, kind, power, square = atoms(box)
        rows = []
        for value in place:
            high, middle, low = pieces(value)
            rows += [high, middle, high, middle, low, high]
        rows += [one, one, one] + list(pieces(square + far[box])) + [zero] * 8
        for k, row in enumerate(rows):
            others[k * ROWS + box * 8 : k * ROWS + box * 8 + 8, :] = row
        high, middle, _ = pieces(power)
        for k, row in enumerate([high, middle, high] + [zero] * 5):
            others_p[k * ROWS + box * 8 : k * ROWS + box * 8 + 8, :] = row
        start[16 * box : 16 * box + 8, :] = -by_kind(kind, [table[4 + k] for k in range(4)])
        start[16 * box + 8 : 16 * box + 16, :] = -one
    place, kind, power, square = atoms(HOME)
    rows = []
    for value in place:
        high, middle, low = pieces(-2.0 * value)
        rows += [high, high, middle, middle, high, low]
    rows += list(pieces(square)) + [one, one, one]
    high, middle, _ = pieces(power)
    rows += [high, high, middle] + [zero] * (W - 27)
    for k, row in enumerate(rows):
        own[k * 8 : k * 8 + 8, :] = row
    diagonal = lax.broadcasted_iota(jnp.int32, (W, W), 0) == lax.broadcasted_iota(
        jnp.int32, (W, W), 1
    )
    floor[0] = jnp.full((W, W), 1e-12, F32)
    floor[1] = jnp.where(diagonal, 2.0, 1e-12)
    blank = jnp.zeros((24, W), BF16)

    def tile(t, carry):
        left = jnp.transpose(own[pl.ds(t, W, stride=8), :])[:, :32].astype(BF16)

        def entry(e, carry):
            row = lists[t, e]
            which = (row >> 4) * TILES + (row & 7)
            right = others[pl.ds(which, 32, stride=ROWS), :].astype(BF16)
            right_p = others_p[pl.ds(which, 8, stride=ROWS), :].astype(BF16)
            right = jnp.concatenate([right, jnp.concatenate([blank, right_p], axis=0)], axis=1)
            both = lax.dot_general(
                left, right, (((1,), (0,)), ((), ())), preferred_element_type=F32
            )
            least = floor[jnp.where(which == HOME * TILES + t, 1, 0)]
            square = jnp.minimum(jnp.maximum(both[:, :W], least), 1.0)
            length = square * lax.rsqrt(square)
            cube = length * square + both[:, W:]
            shield = jnp.exp2(jnp.log2(cube) * (-1.0 / 3.0))
            gap = 1.0 - length
            gap = gap * gap
            shape = (length + 0.5) * (square + 0.2) - 0.05
            blocks[t, e] = (gap * gap) * (shape * shield)
            return carry

        return lax.fori_loop(0, lists.shape[1], entry, carry, unroll=36)

    lax.fori_loop(0, TILES, tile, 0)


def build(lists, far, table, near, edge):
    entries = lists.shape[1]
    return pl.pallas_call(
        functools.partial(build_kernel, edge),
        out_shape=(
            pltpu.VMEM((TILES, entries, W, W), F32),
            jax.ShapeDtypeStruct((27 * 16, W), F32),
        ),
        in_specs=[SMEM, SMEM, SMEM, VMEM],
        out_specs=(VMEM, VMEM),
        scratch_shapes=[
            pltpu.VMEM((32 * ROWS, W), F32),
            pltpu.VMEM((8 * ROWS, W), F32),
            pltpu.VMEM((8 * W, W), F32),
            pltpu.VMEM((2, W, W), F32),
        ],
        compiler_params=pltpu.CompilerParams(vmem_limit_bytes=8 * MIB),
        name="build",
    )(lists, far, table, near)


def spectrum(table, shape):
    values = [jnp.full(shape, table[k], F32) for k in range(4)]
    least = jnp.minimum(jnp.minimum(values[0], values[1]), jnp.minimum(values[2], values[3]))
    most = jnp.maximum(jnp.maximum(values[0], values[1]), jnp.maximum(values[2], values[3]))
    return 0.5 * (least + most) + 1.0, 0.5 * (most - least) + 1.5


def own_lanes():
    shape = (LINES, 8, W)
    return lax.broadcasted_iota(jnp.int32, shape, 2) // 16 == lax.broadcasted_iota(
        jnp.int32, shape, 1
    )


def product_kernel(last, lists, table, around, kinds, blocks, *rest):
    earlier, (out, total, dots) = rest[:-3], rest[-3:]

    def tile(t, carry):
        def entry(e, sums):
            at = lists[t, e]
            block = blocks[t, e].reshape(W // 8, 8, W)
            return tuple(
                sums[k] + block * around[pl.ds(at + 8 * k, 8, stride=0), :][None]
                for k in range(2)
            )

        zero = jnp.zeros((W // 8, 8, W), F32)
        sums = lax.fori_loop(0, lists.shape[1], entry, (zero, zero), unroll=12)
        for k in range(2):
            turned = jnp.transpose(sums[k].reshape(W, W))
            total[pl.ds(t + 8 * k, 1), :] = jnp.sum(turned, axis=0, keepdims=True)
        return carry

    lax.fori_loop(0, TILES, tile, 0)
    kind = kinds[...]
    centre, spread = spectrum(table, (TILES, W))
    eta = by_kind(kind, [table[k] for k in range(4)]) - centre
    home = around[16 * HOME : 16 * HOME + 16, :]
    scale = 20.0 * COULOMB / CUTOFF
    following = (total[...] * scale + jnp.concatenate([eta, eta], axis=0) * home) / (
        jnp.concatenate([spread, spread], axis=0)
    )
    if not last:
        out[...] = following
        return
    basis = [ref[...] for ref in earlier] + [home, following]
    for k in range(2):
        parts = [v[8 * k : 8 * k + 8] for v in basis]
        rows = [parts[i] * parts[j] for i in range(ITERS) for j in range(i, ITERS + 1)] + parts[:ITERS]
        for index, row in enumerate(rows):
            dots[2 * index + k : 2 * index + k + 1, :] = jnp.sum(row, axis=0, keepdims=True)
    dots[2 * ENTRIES :, :] = jnp.zeros((LINES * 8 - 2 * ENTRIES, W), F32)
    folded = dots[...]
    for shift in (64, 32, 16):
        folded = folded + pltpu.roll(folded, shift, 1)
    kept = jnp.where(own_lanes(), folded.reshape(LINES, 8, W), 0.0)
    out[:LINES, :] = jnp.sum(kept, axis=1)
    out[LINES:, :] = jnp.zeros((8 - LINES, W), F32)


def product(lists, table, around, kinds, blocks, earlier=()):
    last = bool(earlier)
    return pl.pallas_call(
        functools.partial(product_kernel, last),
        out_shape=jax.ShapeDtypeStruct((8 if last else 16, W), F32),
        in_specs=[SMEM, SMEM, VMEM, VMEM, VMEM] + [VMEM] * len(earlier),
        out_specs=VMEM,
        scratch_shapes=[pltpu.VMEM((16, W), F32), pltpu.VMEM((LINES * 8, W), F32)],
        compiler_params=pltpu.CompilerParams(vmem_limit_bytes=8 * MIB),
        name="product",
    )(lists, table, around, kinds, blocks, *earlier)


def two_sum(a, b):
    s = a + b
    t = s - a
    return s, (a - (s - t)) + (b - t)


def halves(a):
    t = a * 4097.0
    high = t - (t - a)
    return high, a - high


def add(a, b):
    s, e = two_sum(a[0], b[0])
    return two_sum(s, e + (a[1] + b[1]))


def mul(a, b):
    p = a[0] * b[0]
    ah, al = halves(a[0])
    bh, bl = halves(b[0])
    e = ((ah * bh - p) + ah * bl + al * bh) + al * bl
    return two_sum(p, e + (a[0] * b[1] + a[1] * b[0]))


def neg(a):
    return -a[0], -a[1]


def inverse(a):
    y = 1.0 / a[0]
    guess = (y, jnp.zeros_like(y))
    slip = add((jnp.ones_like(y), jnp.zeros_like(y)), neg(mul(a, guess)))
    return add(guess, mul(guess, slip))


def finish_kernel(table, gram, v0, v1, v2, v3, charges, solutions):
    spread_out = jnp.broadcast_to(gram[:LINES, :][:, None, :], (LINES, 8, W))
    pair = (jnp.where(own_lanes(), spread_out, 0.0).reshape(LINES * 8, W),)
    pair += (jnp.zeros((LINES * 8, W), F32),)
    shift = W // 2
    while shift:
        pair = add(pair, (pltpu.roll(pair[0], shift, 1), pltpu.roll(pair[1], shift, 1)))
        shift //= 2

    def value(index):
        return pair[0][2 * index : 2 * index + 2], pair[1][2 * index : 2 * index + 2]

    index_of = {}
    for i in range(ITERS):
        for j in range(i, ITERS + 1):
            index_of[i, j] = len(index_of)
    dots = {key: value(index) for key, index in index_of.items()}
    sums = [value(len(index_of) + i) for i in range(ITERS)]

    def dot(i, j):
        return dots[min(i, j), max(i, j)]

    none = jnp.zeros((2, W), F32)
    centre, spread = ((value, none) for value in spectrum(table, (2, W)))
    matrix = {
        (i, j): add(mul(spread, dot(i, j + 1)), mul(centre, dot(i, j)))
        for i in range(ITERS)
        for j in range(i + 1)
    }
    size = [abs(matrix[i, i][0]) for i in range(ITERS)]
    right = [dot(i, 0) for i in range(ITERS)]
    inverses, factors = [], {}
    for k in range(ITERS):
        pivot = matrix[k, k]
        usable = abs(pivot[0]) > DROP * size[k]
        turned = inverse((jnp.where(usable, pivot[0], 1.0), jnp.where(usable, pivot[1], 0.0)))
        turned = (jnp.where(usable, turned[0], 0.0), jnp.where(usable, turned[1], 0.0))
        inverses.append(turned)
        for i in range(k + 1, ITERS):
            factors[i, k] = mul(matrix[i, k], turned)
        for i in range(k + 1, ITERS):
            for j in range(k + 1, i + 1):
                matrix[i, j] = add(matrix[i, j], neg(mul(factors[i, k], matrix[j, k])))
            right[i] = add(right[i], neg(mul(factors[i, k], right[k])))
    weights = [None] * ITERS
    for k in reversed(range(ITERS)):
        weight = mul(right[k], inverses[k])
        for i in range(k + 1, ITERS):
            weight = add(weight, neg(mul(factors[i, k], weights[i])))
        weights[k] = weight
    whole = mul(weights[0], sums[0])
    for k in range(1, ITERS):
        whole = add(whole, mul(weights[k], sums[k]))
    basis = [ref[...] for ref in (v0, v1, v2, v3)]
    parts = []
    for k in range(2):
        part = weights[0][0][k : k + 1] * basis[0][8 * k : 8 * k + 8]
        for i in range(1, ITERS):
            part = part + weights[i][0][k : k + 1] * basis[i][8 * k : 8 * k + 8]
        parts.append(part)
        for u in range(TILES):
            solutions[u, k : k + 1, :] = part[u : u + 1]
    level = whole[0][0:1] / whole[0][1:2]
    charges[...] = parts[0] - level * parts[1]


def finish(table, gram, basis):
    return pl.pallas_call(
        finish_kernel,
        out_shape=(jax.ShapeDtypeStruct((TILES, W), F32), jax.ShapeDtypeStruct((TILES, 2, W), F32)),
        in_specs=[SMEM] + [VMEM] * 5,
        out_specs=(VMEM, VMEM),
        compiler_params=pltpu.CompilerParams(vmem_limit_bytes=8 * MIB),
        name="finish",
    )(table, gram, *basis)


def on_device(positions, types, tile_lists, hardness, electroneg, gamma_table):
    atoms = positions.shape[4]
    edge = (atoms * VOLUME) ** (1.0 / 3.0) / CUTOFF
    box = tile_lists // TILES
    place = (box % 3) * 9 + box // 3 % 3 * 3 + box // 9
    rows = place * 2 * TILES + tile_lists % TILES
    inside = jnp.ones((27,), bool)
    for k, axis in enumerate(AXES):
        there = lax.axis_index(axis) + OFFSETS[:, k].astype(np.int32)
        inside = inside & (there >= 0) & (there < lax.axis_size(axis))
    far = jnp.where(inside, 0.0, FAR).astype(F32)
    table = jnp.concatenate([hardness, electroneg, gamma_table])
    kinds = types.reshape(TILES, W).astype(F32)
    cells = jnp.concatenate([positions.reshape(3 * TILES, W), kinds], axis=0)
    near = surrounded(cells)
    blocks, start = build(rows, far, table, near, edge)
    basis = [start[16 * HOME : 16 * HOME + 16]]
    around = start
    for _ in range(ITERS - 1):
        basis.append(product(rows, table, around, kinds, blocks))
        around = surrounded(basis[-1]).reshape(27 * 16, W)
    gram = summed(product(rows, table, around, kinds, blocks, tuple(basis[:-1])))
    charges, solutions = finish(table, gram, basis)
    solutions = jnp.transpose(solutions, (1, 0, 2)).reshape(1, 1, 1, 2, atoms)
    return charges.reshape(1, 1, 1, atoms), solutions


def solution(mesh):
    names = ("y_low", "core", "y_high", "x", "gz")
    split = Mesh(mesh.devices.reshape(2, 2, 2, 4, mesh.shape["gz"]), names)
    return jax.shard_map(
        on_device,
        mesh=split,
        in_specs=(P(*AXES, None, None), P(*AXES, None), P(), P(), P(), P()),
        out_specs=(P(*AXES, None), P(*AXES, None, None)),
        check_vma=False,
    )
```
